128 devices in a mesh: seq: 16 (over y, x_lo, core), tp: 8 (over z, x_hi).
Axes of the slice: x: 4 (x_hi: 2, x_lo: 2; x = x_hi * 2 + x_lo), y: 4, z: 4, core: 2. Of those that a mesh axis runs over, the one named last changes fastest.
Arguments:
- tokens: bfloat16 [8192, 1024], P('seq', 'tp'), may hold values from -6 to 6
- variate: int32 [8192], P('seq'), may hold values from 0 to 3
- positions: int32 [8192], P('seq'), may hold values from 0 to 511
- lengths: int32 [4], replicated, may hold values from 1 to 4096, 8192 in all
- page_table: int32 [144], replicated, may hold values from 0 to 143, each once
- gain_attn: bfloat16 [1024], replicated, may hold values from 0.099609375 to 1.8984375
- w_query: bfloat16 [1024, 1024], P(None, 'tp'), may hold values from -1 to 1
- w_key: bfloat16 [1024, 1024], P(None, 'tp'), may hold values from -1 to 1
- w_value: bfloat16 [1024, 1024], P(None, 'tp'), may hold values from -0.1875 to 0.1875
- var_bias: float32 [2, 16], P(None, 'tp'), may hold values from -2 to 2
- w_out: bfloat16 [1024, 1024], P('tp'), may hold values from -0.1875 to 0.1875
- gain_ffn: bfloat16 [1024], replicated, may hold values from 0.099609375 to 1.8984375
- w_gate: bfloat16 [1024, 4096], P(None, 'tp'), may hold values from -0.1875 to 0.1875
- w_up: bfloat16 [1024, 4096], P(None, 'tp'), may hold values from -0.1875 to 0.1875
- w_down: bfloat16 [4096, 1024], P('tp'), may hold values from -0.09375 to 0.09375
Outputs:
- mixed: bfloat16 [8192, 1024], P('seq', 'tp')
- cache: bfloat16 [9216, 2, 1024], P('seq', None, 'tp')
The draws below stay inside these ranges and needn't reach their ends.
Inputs may be any that keep to these rules, and one draw needn't show every extreme that they name: The lengths fill all 8192 token positions in order; some request has exactly 4096 tokens. `page_table`: each physical page appears once.
All inputs are finite; a program needn't handle non-finite values.
Results may differ from the reference program's by a relative error of at most 0.018.
Values may be sent and summed in bfloat16 or wider, within the bound.
A program may use at most 64 MiB of HBM per device.

```python
import math
import jax
import jax.numpy as jnp
import numpy as np
from jax import lax

D = 1024
HD = 64
FF = 4096
TOK_DEV = 512
PAGE = 64
VARS = 4
TIMES = 512
HEADS = 16
TOKENS = 8192
LEN_MAX = 4096
REQS = 4
PAGES = 144
CACHE_ROWS = 9216


def query_key_pair(key):
    own_query = jax.random.normal(jax.random.fold_in(key, 11), (D, HEADS * HD), jnp.float32)
    own_key = jax.random.normal(jax.random.fold_in(key, 13), (D, HEADS * HD), jnp.float32)
    scale = D ** (-0.5)
    query_part = own_query * scale
    key_part = own_key * scale
    limit = 32.0 * scale
    return (jnp.clip(query_part, -limit, limit), jnp.clip(key_part, -limit, limit))


def draw_w_query(key, part):
    return query_key_pair(key)[0].astype(jnp.bfloat16)


def draw_w_key(key, part):
    return query_key_pair(key)[1].astype(jnp.bfloat16)


def touch_ends(drawn, key, smallest, high):
    shape = drawn.shape
    spot = [jax.random.randint(jax.random.fold_in(key, axis), (), 0, shape[axis]) for axis in range(len(shape))]
    drawn = drawn.at[tuple(spot)].set(smallest)
    longest = shape.index(max(shape))
    spot[longest] = (spot[longest] + 1) % shape[longest]
    return drawn.at[tuple(spot)].set(high)


def levels(key, dims, shards, least, high):
    def one(axis_at, shards_of):
        steps = jax.random.uniform(jax.random.fold_in(jax.random.fold_in(key, 6), axis_at), (shards_of,), jnp.float32, least / len(shards), high / len(shards))
        return jnp.repeat(jnp.exp(steps), dims[axis_at] // shards_of).reshape((-1,) + (1,) * (len(dims) - axis_at - 1))

    level = one(*shards[0])
    for cut in shards[1:]:
        level = level * one(*cut)
    return level


def length_profile(amount, total, most, slope):
    portions = [(1 << 20) // math.isqrt(rank ** slope) + 1 for rank in range(2, amount + 1)]
    rest, counts = total - most - (amount - 1), [1] * (amount - 1)
    while rest > 0:
        free = [i for i in range(amount - 1) if counts[i] < most]
        whole, left = sum([portions[i] for i in free]), rest
        for i in free:
            more = min(most - counts[i], max(1, left * portions[i] // whole), rest)
            counts[i] = counts[i] + more
            rest = rest - more
    return np.array([most] + counts)


def ragged_sizes(key, number_of, total, most, lean):
    if number_of == 2:
        one = jax.random.randint(key, (), max(1, total - most), min(most, total - 1) + 1)
        return jnp.stack([one, total - one])
    sizes = jnp.asarray(length_profile(number_of, total, most, lean), jnp.int32)
    twos = (number_of - 1) // 2
    donor, receiver = sizes[1:1 + 2 * twos:2], sizes[2:2 + 2 * twos:2]
    margin = jnp.minimum(donor - 1, most - receiver)
    shifted = jax.random.randint(jax.random.fold_in(key, 1), (twos,), 0, 1 << 20) % (margin + 1)
    sizes = sizes.at[1:1 + 2 * twos:2].set(donor - shifted).at[2:2 + 2 * twos:2].set(receiver + shifted)
    return sizes[jax.random.permutation(jax.random.fold_in(key, 2), number_of)]


def bell_draw(stream_key, shape, width, reach, pieces=(), kind=jnp.bfloat16):
    loudness = levels(stream_key, shape, pieces, -0.22, 0.18) if pieces else 1.0
    drawn = jax.random.normal(stream_key, shape, jnp.float32) * width * loudness
    return jnp.minimum(jnp.maximum(drawn, -reach), reach).astype(kind)


def setup_inputs(seed: int = 0) -> dict:
    seeds = jax.random.split(jax.random.key(seed), 16)
    return {
        "tokens": bell_draw(seeds[0], (TOKENS, D), 1.0, 6.0, ((0, 16), (1, 8))),
        "variate": touch_ends(jax.random.randint(seeds[1], (TOKENS,), 0, VARS), jax.random.fold_in(seeds[1], 1), 0, VARS - 1).astype(jnp.int32),
        "positions": touch_ends(jax.random.randint(seeds[2], (TOKENS,), 0, TIMES), jax.random.fold_in(seeds[2], 1), 0, TIMES - 1).astype(jnp.int32),
        "lengths": ragged_sizes(seeds[3], REQS, TOKENS, LEN_MAX, 2).astype(jnp.int32),
        "page_table": jax.random.permutation(seeds[4], PAGES).astype(jnp.int32),
        "gain_attn": jnp.clip(1.0 + 0.18 * jax.random.normal(seeds[5], (D,), jnp.float32), 0.099609375, 1.8984375).astype(jnp.bfloat16),
        "w_query": draw_w_query(jax.random.fold_in(seeds[15], 71), 0),
        "w_key": draw_w_key(jax.random.fold_in(seeds[15], 71), 0),
        "w_value": bell_draw(seeds[8], (D, HEADS * HD), D ** -0.5, 0.1875, ((1, 8),)),
        "var_bias": jnp.clip(jax.random.uniform(seeds[9], (2, HEADS), jnp.float32, -2.0, 2.0) * levels(seeds[9], (2, HEADS), ((1, 8),), -0.4, 0.0), -2.0, 2.0),
        "w_out": bell_draw(seeds[10], (HEADS * HD, D), (HEADS * HD) ** -0.5, 0.1875, ((0, 8),)),
        "gain_ffn": jnp.clip(1.0 + 0.18 * jax.random.normal(seeds[11], (D,), jnp.float32), 0.099609375, 1.8984375).astype(jnp.bfloat16),
        "w_gate": bell_draw(seeds[12], (D, FF), D ** -0.5, 0.1875, ((1, 8),)),
        "w_up": bell_draw(seeds[13], (D, FF), D ** -0.5, 0.1875, ((1, 8),)),
        "w_down": bell_draw(seeds[14], (FF, D), FF ** -0.5, 0.09375, ((0, 8),)),
    }


def root_mean_norm(values, gain):
    values = values.astype(jnp.float32)
    scale = lax.rsqrt(lax.optimization_barrier(jnp.mean(values * values, axis=-1, keepdims=True)) + 1e-06)
    return values * scale * gain.astype(jnp.float32)

def rotate(vectors, positions):
    half_dim = vectors.shape[-1] // 2
    frequency = 10000.0 ** (-jnp.arange(half_dim, dtype=jnp.float32) / half_dim)
    angles = positions.astype(jnp.float32)[:, None] * frequency[None, :]
    cosine = jnp.cos(angles)[:, None, :]
    sine_part = jnp.sin(angles)[:, None, :]
    first_half = vectors[..., :half_dim]
    second_half = vectors[..., half_dim:]
    return jnp.concatenate([first_half * cosine - second_half * sine_part, second_half * cosine + first_half * sine_part], axis=-1)

def segment_of(index, request_ends):
    return lax.optimization_barrier(jnp.sum((index[:, None] >= request_ends[None, :]).astype(jnp.int32), axis=1)).astype(jnp.int32)

def cache_slots(lengths, page_table, index):
    request_ends = jnp.cumsum(lengths).astype(jnp.int32)
    request_starts = request_ends - lengths
    page_counts = (lengths + PAGE - 1) // PAGE
    page_bases = jnp.cumsum(page_counts).astype(jnp.int32) - page_counts
    segment = segment_of(index, request_ends)
    chosen = segment[:, None] == jnp.arange(lengths.shape[0], dtype=jnp.int32)[None, :]
    offset_in = index - lax.optimization_barrier(jnp.sum(jnp.where(chosen, request_starts[None, :], 0), axis=1)).astype(jnp.int32)
    logical = lax.optimization_barrier(jnp.sum(jnp.where(chosen, page_bases[None, :], 0), axis=1)).astype(jnp.int32) + offset_in // PAGE
    page_ids = jnp.arange(page_table.shape[0], dtype=jnp.int32)
    physical = lax.optimization_barrier(jnp.sum(jnp.where(logical[:, None] == page_ids[None, :], page_table[None, :], 0), axis=1)).astype(jnp.int32)
    return physical * PAGE + offset_in % PAGE

def reference(tokens, variate, positions, lengths, page_table, gain_attn, w_query, w_key, w_value, var_bias, w_out, gain_ffn, w_gate, w_up, w_down):
    index = jnp.arange(TOKENS, dtype=jnp.int32)
    normed = root_mean_norm(tokens, gain_attn).astype(jnp.bfloat16)
    query_rows = rotate(jnp.dot(normed, w_query, preferred_element_type=jnp.float32).reshape(TOKENS, HEADS, HD), positions).astype(jnp.bfloat16)
    key_rows = rotate(jnp.dot(normed, w_key, preferred_element_type=jnp.float32).reshape(TOKENS, HEADS, HD), positions).astype(jnp.bfloat16)
    value_rows = jnp.dot(normed, w_value, preferred_element_type=jnp.float32).astype(jnp.bfloat16).reshape(TOKENS, HEADS, HD)
    request_ends = jnp.cumsum(lengths).astype(jnp.int32)
    segment = segment_of(index, request_ends)
    window = min(LEN_MAX + TOK_DEV, TOKENS)

    def one_block(block):
        first = (block * TOK_DEV).astype(jnp.int32)
        key_first = jnp.clip(first + TOK_DEV - window, 0, TOKENS - window).astype(jnp.int32)
        query_block = lax.dynamic_slice_in_dim(query_rows, first, TOK_DEV, 0).astype(jnp.float32)
        key_block = lax.dynamic_slice_in_dim(key_rows, key_first, window, 0).astype(jnp.float32)
        value_block = lax.dynamic_slice_in_dim(value_rows, key_first, window, 0).astype(jnp.float32)
        query_index = first + jnp.arange(TOK_DEV, dtype=jnp.int32)
        key_index = key_first + jnp.arange(window, dtype=jnp.int32)
        query_segment = lax.dynamic_slice_in_dim(segment, first, TOK_DEV, 0)
        key_segment = lax.dynamic_slice_in_dim(segment, key_first, window, 0)
        query_variate = lax.dynamic_slice_in_dim(variate, first, TOK_DEV, 0)
        key_variate = lax.dynamic_slice_in_dim(variate, key_first, window, 0)
        scores = jnp.einsum('qhd,khd->hqk', query_block, key_block) * HD ** (-0.5)
        same = query_variate[:, None] == key_variate[None, :]
        scores = scores + jnp.where(same[None], var_bias[0][:, None, None], var_bias[1][:, None, None])
        visible = (query_segment[:, None] == key_segment[None, :]) & (query_index[:, None] >= key_index[None, :])
        scores = jnp.where(visible[None], scores, -1e+30)
        peak = lax.optimization_barrier(jnp.max(scores, axis=-1, keepdims=True))
        weights = jnp.where(visible[None], jnp.exp(scores - peak), 0.0)
        totals = lax.optimization_barrier(jnp.sum(weights, axis=-1))
        rounded = lax.optimization_barrier(weights.astype(jnp.bfloat16)).astype(jnp.float32)
        summed = jnp.einsum('hqk,khd->qhd', rounded, value_block) / jnp.transpose(totals)[:, :, None]
        return summed.reshape(TOK_DEV, HEADS * HD).astype(jnp.bfloat16)
    attended = lax.map(one_block, jnp.arange(TOKENS // TOK_DEV, dtype=jnp.int32)).reshape(TOKENS, HEADS * HD)
    projected = jnp.dot(attended, w_out, preferred_element_type=jnp.float32)
    residual = (tokens.astype(jnp.float32) + projected).astype(jnp.bfloat16)
    normed_mid = root_mean_norm(residual, gain_ffn).astype(jnp.bfloat16)
    gate_part = jnp.dot(normed_mid, w_gate, preferred_element_type=jnp.float32)
    up_part = jnp.dot(normed_mid, w_up, preferred_element_type=jnp.float32)
    hidden = (jax.nn.silu(gate_part) * up_part).astype(jnp.bfloat16)
    mixed = (residual.astype(jnp.float32) + jnp.dot(hidden, w_down, preferred_element_type=jnp.float32)).astype(jnp.bfloat16)
    stacked = jnp.stack([key_rows.reshape(TOKENS, HEADS * HD), value_rows.reshape(TOKENS, HEADS * HD)], axis=1)
    slots = cache_slots(lengths, page_table, index)
    cache = jnp.zeros((CACHE_ROWS, 2, HEADS * HD), jnp.bfloat16).at[slots].set(stacked)
    return (mixed, cache)
```

```python
import functools

import jax
import jax.numpy as jnp
from jax import lax
from jax.experimental import pallas as pl
from jax.experimental.pallas import tpu as pltpu
from jax.sharding import PartitionSpec as P

MESH = pl.DeviceIdType.MESH
F32 = jnp.float32
BF16 = jnp.bfloat16
NEG = -1e30

T = 512
LANES = 128
CH = 4
KX = 144
N_SEQ = 16
N_TP = 8
PAGE = 64
PAGES_DEV = 9
PAGES = 144
REQS = 4


class Gather:
    COUNT = 14

    def __init__(self, own, part, slot, ring, pair, to_next, to_prev, to_pair, sems, base):
        self.own, self.part, self.slot = own, part, slot
        self.ring, self.pair = ring, pair
        self.targets = {"next": to_next, "prev": to_prev, "pair": to_pair}
        self.send, self.recv = sems
        self.base = base
        self.sent = []

    def at(self, dr, flip):
        ring = lax.rem(self.ring + (dr + 4), 4)
        return self.slot(ring, 1 - self.pair if flip else self.pair)

    def push(self, k, source, place, which, target):
        copy = pltpu.make_async_remote_copy(
            src_ref=source,
            dst_ref=self.part(place, which),
            send_sem=self.send.at[self.base + k],
            recv_sem=self.recv.at[self.base + k],
            device_id=self.targets[target],
            device_id_type=MESH,
        )
        copy.start()
        self.sent.append(copy)

    def wait(self, k, dr, flip, which):
        ref = self.part(self.at(dr, flip), which)
        pltpu.make_async_remote_copy(
            src_ref=ref,
            dst_ref=ref,
            send_sem=self.send.at[self.base + k],
            recv_sem=self.recv.at[self.base + k],
            device_id=self.targets["pair"],
            device_id_type=MESH,
        ).wait_recv()

    def start(self):
        mine = self.at(0, False)
        for which in (0, 1):
            self.push(which, self.own(which), mine, which, "pair")
        for which in (0, 1):
            self.push(2 + which, self.own(which), mine, which, "next")
            self.push(5 - which, self.own(1 - which), mine, 1 - which, "prev")

    def relay_pair(self):
        place = self.at(0, True)
        self.wait(0, 0, True, 0)
        self.wait(1, 0, True, 1)
        for which in (0, 1):
            self.push(6 + which, self.part(place, which), place, which, "next")
            self.push(9 - which, self.part(place, 1 - which), place, 1 - which, "prev")

    def relay_ring(self, flip):
        first = 6 if flip else 2
        onward = 12 if flip else 10
        before, after = self.at(-1, flip), self.at(1, flip)
        self.wait(first, -1, flip, 0)
        self.push(onward, self.part(before, 0), before, 0, "next")
        self.wait(first + 3, 1, flip, 1)
        self.push(onward + 1, self.part(after, 1), after, 1, "prev")
        self.wait(first + 1, -1, flip, 1)
        self.wait(first + 2, 1, flip, 0)

    def finish(self, flip):
        onward = 12 if flip else 10
        self.wait(onward, 2, flip, 0)
        self.wait(onward + 1, 2, flip, 1)

    def drain(self):
        for copy in self.sent:
            copy.wait_send()


def spread(row):
    return jnp.broadcast_to(row, (LANES, LANES)).T


def kernel(
    lengths,
    page_table,
    var_bias,
    tokens,
    variate,
    positions,
    frequency,
    gain_attn,
    gain_ffn,
    w_query,
    w_key,
    w_value,
    w_out,
    w_gate,
    w_up,
    w_down,
    mixed,
    k_all,
    v_all,
    tok_buf,
    w_qkv,
    kbuf,
    vbuf,
    qbuf,
    peak,
    acc,
    wout_buf,
    att_own,
    att_buf,
    res_buf,
    normed_buf,
    gate_buf,
    up_buf,
    down_buf,
    part_buf,
    hop_buf,
    near_buf,
    sum_buf,
    pair_tx,
    pair_rx,
    table,
    send_sem,
    recv_sem,
    load_sem,
):
    sems = (send_sem, recv_sem)
    me = lax.axis_index("seq")
    tp = lax.axis_index("tp")
    y, xl, core = me // 4, lax.rem(me // 2, 2), lax.rem(me, 2)
    z, xh = tp // 2, lax.rem(tp, 2)

    def seq_of(ys, xs, cs):
        return ys * 4 + xs * 2 + cs

    tp_at = lambda t: {"seq": me, "tp": t}
    seq_at = lambda s: {"seq": s, "tp": tp}
    z_next, z_prev = lax.rem(z + 1, 4), lax.rem(z + 3, 4)
    y_next, y_prev = lax.rem(y + 1, 4), lax.rem(y + 3, 4)

    loads = [
        pltpu.make_async_copy(w_query, w_qkv.at[:, pl.ds(0, 128)], load_sem.at[0]),
        pltpu.make_async_copy(w_key, w_qkv.at[:, pl.ds(128, 128)], load_sem.at[1]),
        pltpu.make_async_copy(w_value, w_qkv.at[:, pl.ds(256, 128)], load_sem.at[2]),
        pltpu.make_async_copy(w_gate, gate_buf, load_sem.at[3]),
        pltpu.make_async_copy(w_up, up_buf, load_sem.at[4]),
        pltpu.make_async_copy(w_down, down_buf, load_sem.at[5]),
    ]
    for load in loads:
        load.start()

    barrier = pltpu.get_barrier_semaphore()
    peers = [tp_at(lax.rem(tp + d, N_TP)) for d in range(1, N_TP)]
    peers += [
        seq_at(seq_of(y, xl, 1 - core)),
        seq_at(seq_of(y, 1 - xl, core)),
        seq_at(seq_of(y_next, xl, core)),
        seq_at(seq_of(y_prev, xl, core)),
    ]
    for peer in peers:
        pl.semaphore_signal(barrier, inc=1, device_id=peer, device_id_type=MESH)
    pl.semaphore_wait(barrier, len(peers))

    tp_targets = (tp_at(z_next * 2 + xh), tp_at(z_prev * 2 + xh), tp_at(z * 2 + 1 - xh))
    tp_slot = lambda r, p: r * 2 + p

    tok = Gather(
        lambda w: tokens.at[pl.ds(w * 256, 256)],
        lambda s, w: tok_buf.at[s, pl.ds(w * 256, 256)],
        tp_slot, z, xh, *tp_targets, sems, 0,
    )
    tok.start()
    tok_buf[tp] = tokens[...]

    lane = lax.broadcasted_iota(jnp.int32, (LANES, LANES), 1)
    low = lax.rem(lane, 64) < 32
    for c in range(CH):
        angles = spread(positions[pl.ds(c, 1), :].astype(F32)) * frequency[...]
        rows = pl.ds(c * 128, 128)
        table[0, rows, :] = jnp.cos(angles)
        sine = jnp.sin(angles)
        table[1, rows, :] = jnp.where(low, -sine, sine)

    tok.relay_pair()
    tok.relay_ring(False)
    tok.relay_ring(True)
    tok.finish(False)
    tok.finish(True)
    for load in loads[:3]:
        load.wait()

    ends = []
    total = jnp.int32(0)
    for r in range(REQS):
        total = total + lengths[r]
        ends.append(total)
    gains = [gain_attn[:, pl.ds(t * 128, 128)].astype(F32) for t in range(N_TP)]

    def segments(index):
        count = jnp.zeros(index.shape, jnp.int32)
        for end in ends:
            count += jnp.where(index >= end, 1, 0)
        return count

    sub16 = lax.broadcasted_iota(jnp.int32, (16, LANES), 0)
    lane16 = lax.broadcasted_iota(jnp.int32, (16, LANES), 1)
    sub = lax.broadcasted_iota(jnp.int32, (LANES, LANES), 0)
    first_head = lane < 64

    def project(c, _):
        rows = pl.ds(pl.multiple_of(c * 128, 128), 128)
        blocks = [tok_buf[t, rows, :].astype(F32) for t in range(N_TP)]
        squares = blocks[0] * blocks[0]
        for block in blocks[1:]:
            squares += block * block
        scale = lax.rsqrt(jnp.sum(squares, axis=1, keepdims=True) * (1.0 / 1024) + 1e-6)
        normed = jnp.concatenate([(b * scale * g).astype(BF16) for b, g in zip(blocks, gains)], axis=1)
        out = jnp.dot(normed, w_qkv[...], preferred_element_type=F32)
        cosine, sine = table[0, rows, :], table[1, rows, :]

        def rope(u):
            partner = jnp.where(low, pltpu.roll(u, 96, 1), pltpu.roll(u, 32, 1))
            return (u * cosine + partner * sine).astype(BF16)

        query = rope(out[:, :128]).astype(F32) * 0.125
        keys = rope(out[:, 128:256])
        kbuf[me, c, pl.ds(0, 128), :] = keys.astype(F32).T.astype(BF16)
        vbuf[pl.ds(pl.multiple_of(me * T + c * 128, 128), 128), :] = out[:, 256:].astype(BF16)

        vrow = variate[pl.ds(c, 1), :]
        kseg = segments(me * T + c * 128 + lane16)
        vb = jnp.broadcast_to(vrow, (16, LANES))
        code = jnp.where(sub16 < 8, lax.rem(sub16, 4) - vb, kseg + 8 - sub16)
        kbuf[me, c, pl.ds(128, 16), :] = jnp.where(code == 0, 1.0, 0.0).astype(BF16)

        vcol = spread(vrow.astype(F32)).astype(jnp.int32)
        qseg = segments(me * T + c * 128 + sub)
        seg_part = jnp.where(qseg == lane - 8, 0.0, jnp.where(lane < 12, NEG, 0.0))
        for h in range(2):
            weight = jnp.where(vcol == lax.rem(lane, 4), var_bias[0, h], var_bias[1, h])
            head = weight.astype(BF16).astype(F32)
            extra = jnp.where(lane < 4, head, jnp.where(lane < 8, weight - head, seg_part))
            own = first_head if h == 0 else jnp.logical_not(first_head)
            place = pl.ds(pl.multiple_of(h * T + c * 128, 128), 128)
            qbuf[place, pl.ds(0, 128)] = jnp.where(own, query, 0.0).astype(BF16)
            qbuf[place, pl.ds(128, 16)] = extra[:, :16].astype(BF16)
        return 0

    lax.fori_loop(0, CH, project, 0)

    def kv_part(s, w):
        return kbuf.at[s] if w == 0 else vbuf.at[pl.ds(pl.multiple_of(s * T, T), T)]

    kv = Gather(
        lambda w: kv_part(me, w), kv_part,
        lambda r, p: seq_of(r, p, core), y, xl,
        seq_at(seq_of(y_next, xl, core)), seq_at(seq_of(y_prev, xl, core)), seq_at(seq_of(y, 1 - xl, core)),
        sems, 14,
    )
    core_base = 28
    core_sent = []

    def core_copy(k, s, w):
        ref = kv_part(s, w)
        return pltpu.make_async_remote_copy(
            src_ref=ref, dst_ref=ref,
            send_sem=send_sem.at[core_base + k], recv_sem=recv_sem.at[core_base + k],
            device_id=seq_at(seq_of(y, xl, 1 - core)), device_id_type=MESH,
        )

    order = [(0, False), (0, True), (-1, False), (1, False), (-1, True), (1, True), (2, False), (2, True)]

    def place_of(dr, flip, cs):
        return seq_of(lax.rem(y + dr + 4, 4), (1 - xl) if flip else xl, cs)

    def core_send(n):
        s = place_of(*order[n], core)
        for w in (0, 1):
            copy = core_copy(n * 2 + w, s, w)
            copy.start()
            core_sent.append(copy)

    def core_wait(n):
        s = place_of(*order[n], 1 - core)
        for w in (0, 1):
            core_copy(n * 2 + w, s, w).wait_recv()

    core_send(0)
    kv.start()

    wo = Gather(
        lambda w: w_out.at[pl.ds(w * 64, 64)],
        lambda s, w: wout_buf.at[s, pl.ds(w * 64, 64)],
        tp_slot, z, xh, *tp_targets, sems, 44,
    )
    wo.start()
    wout_buf[tp] = w_out[...]

    ones = jnp.ones((T, LANES), BF16)

    def attend(s, diagonal):
        keys = jnp.concatenate([kbuf[s, c] for c in range(CH)], axis=1)
        values = jnp.concatenate([vbuf[pl.ds(pl.multiple_of(s * T, T), T), :], ones], axis=1)

        def tile(i, _):
            for h in range(2):
                rows = pl.ds(pl.multiple_of(h * T + i * 128, 128), 128)
                score = jnp.dot(qbuf[rows, :], keys, preferred_element_type=F32)
                if diagonal:
                    qi = i * 128 + lax.broadcasted_iota(jnp.int32, (128, T), 0)
                    ki = lax.broadcasted_iota(jnp.int32, (128, T), 1)
                    score = jnp.where(ki <= qi, score, NEG)
                    top = jnp.broadcast_to(jnp.max(score, axis=1, keepdims=True), (128, LANES))
                else:
                    before = peak[rows, :]
                    top = jnp.maximum(before, jnp.max(score, axis=1, keepdims=True))
                weight = jnp.exp(score - jnp.concatenate([top] * CH, axis=1)).astype(BF16)
                product = jnp.dot(weight, values, preferred_element_type=F32)
                if not diagonal:
                    fade = jnp.exp(before - top)
                    product += acc[rows, :] * jnp.concatenate([fade, fade], axis=1)
                acc[rows, :] = product
                peak[rows, :] = top
            return 0

        lax.fori_loop(0, CH, tile, 0)

    def attend_if(n, cs):
        s = place_of(*order[n], cs)

        @pl.when(jnp.logical_and(s < me, s >= me - 8))
        def _():
            attend(s, False)

    attend(me, True)
    core_wait(0)
    attend_if(0, 1 - core)
    kv.relay_pair()
    core_send(1)
    kv.relay_ring(False)
    core_send(2)
    core_send(3)
    wo.relay_pair()
    attend_if(1, core)
    attend_if(2, core)
    core_wait(1)
    core_wait(2)
    core_wait(3)
    wo.relay_ring(False)
    attend_if(1, 1 - core)
    attend_if(2, 1 - core)
    kv.relay_ring(True)
    core_send(4)
    core_send(5)
    wo.relay_ring(True)
    attend_if(4, core)
    kv.finish(False)
    core_send(6)
    core_wait(4)
    core_wait(5)
    attend_if(4, 1 - core)
    attend_if(6, core)
    kv.finish(True)
    core_send(7)
    core_wait(6)
    attend_if(6, 1 - core)
    attend_if(7, core)
    core_wait(7)
    attend_if(7, 1 - core)

    stores = [
        pltpu.make_async_copy(kbuf, k_all, load_sem.at[6]),
        pltpu.make_async_copy(vbuf, v_all, load_sem.at[7]),
    ]
    for store in stores:
        store.start()

    for c in range(CH):
        low_rows, high_rows = pl.ds(c * 128, 128), pl.ds(T + c * 128, 128)
        a, b = acc[low_rows, :], acc[high_rows, :]
        att = jnp.where(first_head, a[:, :128] / a[:, 128:], b[:, :128] / b[:, 128:]).astype(BF16)
        att_own[pl.ds(2 * c, 2)] = att.reshape(2, 64, 128)
    swap_base = 58
    swaps = []

    def swap(d, target, source_slot, place):
        return pltpu.make_async_remote_copy(
            src_ref=att_own.at[source_slot], dst_ref=att_buf.at[place],
            send_sem=send_sem.at[swap_base + d], recv_sem=recv_sem.at[swap_base + d],
            device_id=tp_at(target), device_id_type=MESH,
        )

    for d in (4, 3, 5, 2, 6, 1, 7):
        target = lax.rem(tp + d, N_TP)
        copy = swap(d, target, target, tp)
        copy.start()
        swaps.append(copy)
    att_buf[tp] = att_own[tp]
    wo.finish(False)
    wo.finish(True)
    for d in range(1, N_TP):
        origin = lax.rem(tp - d + N_TP, N_TP)
        swap(d, origin, origin, origin).wait_recv()
    rows_att = jnp.concatenate([att_buf[t] for t in range(N_TP)], axis=1)
    projected = jnp.dot(rows_att, wout_buf[...].reshape(1024, 1024), preferred_element_type=F32)
    own_rows = pl.ds(pl.multiple_of(tp * 64, 64), 64)
    own_tokens = jnp.concatenate([tok_buf[t, own_rows, :] for t in range(N_TP)], axis=1)
    res_buf[tp] = (own_tokens.astype(F32) + projected).astype(BF16)

    res = Gather(
        lambda w: res_buf.at[tp, pl.ds(w * 32, 32)],
        lambda s, w: res_buf.at[s, pl.ds(w * 32, 32)],
        tp_slot, z, xh, *tp_targets, sems, 66,
    )
    res.start()
    res.relay_pair()
    res.relay_ring(False)
    res.relay_ring(True)
    res.finish(False)
    res.finish(True)
    for load in loads[3:]:
        load.wait()

    def normalise(s, _):
        x = res_buf[s].astype(F32)
        scale = lax.rsqrt(jnp.sum(x * x, axis=1, keepdims=True) * (1.0 / 1024) + 1e-6)
        normed_buf[pl.ds(pl.multiple_of(s * 64, 64), 64), :] = (x * scale * gain_ffn[...].astype(F32)).astype(BF16)
        return 0

    lax.fori_loop(0, N_TP, normalise, 0)

    ring_base = 80
    ring_sent = []

    def ring_copy(k, source, place, target):
        return pltpu.make_async_remote_copy(
            src_ref=source, dst_ref=place,
            send_sem=send_sem.at[ring_base + k], recv_sem=recv_sem.at[ring_base + k],
            device_id=target, device_id_type=MESH,
        )

    def ring_start(k, source, place, target):
        copy = ring_copy(k, source, place, target)
        copy.start()
        ring_sent.append(copy)

    z_far = lax.rem(z + 2, 4)
    next_at, prev_at, pair_at = tp_targets

    def pieces(zs, j, half):
        return part_buf.at[pl.ds(zs * 2, 2), pl.ds(j * 256 + half * 128, 128)]

    def ffn(j):
        rows = pl.ds(j * 256, 256)
        x = normed_buf[rows, :]
        gate = jnp.dot(x, gate_buf[...], preferred_element_type=F32)
        up = jnp.dot(x, up_buf[...], preferred_element_type=F32)
        hidden = (gate * (1.0 / (1.0 + jnp.exp(-gate))) * up).astype(BF16)
        for t in range(N_TP):
            part_buf[t, rows, :] = jnp.dot(
                hidden, down_buf[:, pl.ds(t * 128, 128)], preferred_element_type=F32
            ).astype(BF16)

    def ring_first(j):
        k = j * 8
        ring_start(k, pieces(z_far, j, 0), hop_buf.at[j, 0], next_at)
        ring_start(k + 1, pieces(z_far, j, 1), hop_buf.at[j, 1], prev_at)
        ring_start(k + 2, pieces(z_next, j, 1), near_buf.at[j, 0, 1], next_at)
        ring_start(k + 3, pieces(z_prev, j, 0), near_buf.at[j, 1, 0], prev_at)

    def ring_second(j):
        k = j * 8
        ring_copy(k, hop_buf.at[j, 0], hop_buf.at[j, 0], next_at).wait_recv()
        sum_buf[j, 0] = (hop_buf[j, 0].astype(F32) + pieces(z_next, j, 0)[...].astype(F32)).astype(BF16)
        ring_start(k + 4, sum_buf.at[j, 0], near_buf.at[j, 0, 0], next_at)
        ring_copy(k + 1, hop_buf.at[j, 1], hop_buf.at[j, 1], prev_at).wait_recv()
        sum_buf[j, 1] = (hop_buf[j, 1].astype(F32) + pieces(z_prev, j, 1)[...].astype(F32)).astype(BF16)
        ring_start(k + 5, sum_buf.at[j, 1], near_buf.at[j, 1, 1], prev_at)

    def own_sum(j, xs):
        total = []
        for half in (0, 1):
            own = part_buf[z * 2 + xs, pl.ds(j * 256 + half * 128, 128), :].astype(F32)
            total.append(own + near_buf[j, 0, half, xs].astype(F32) + near_buf[j, 1, half, xs].astype(F32))
        return jnp.concatenate(total, axis=0)

    def ring_third(j):
        k = j * 8
        ring_copy(k + 2, near_buf.at[j, 0, 1], near_buf.at[j, 0, 1], next_at).wait_recv()
        ring_copy(k + 3, near_buf.at[j, 1, 0], near_buf.at[j, 1, 0], prev_at).wait_recv()
        ring_copy(k + 4, near_buf.at[j, 0, 0], near_buf.at[j, 0, 0], next_at).wait_recv()
        ring_copy(k + 5, near_buf.at[j, 1, 1], near_buf.at[j, 1, 1], prev_at).wait_recv()
        pair_tx[j] = own_sum(j, 1 - xh).astype(BF16)
        ring_start(k + 6, pair_tx.at[j], pair_rx.at[j], pair_at)

    def ring_last(j):
        ring_copy(j * 8 + 6, pair_rx.at[j], pair_rx.at[j], pair_at).wait_recv()
        columns = pl.ds(pl.multiple_of(tp * 128, 128), 128)
        kept = jnp.concatenate([res_buf[4 * j + i, :, columns] for i in range(4)], axis=0).astype(F32)
        mixed[pl.ds(j * 256, 256), :] = (kept + own_sum(j, xh) + pair_rx[j].astype(F32)).astype(BF16)

    ffn(0)
    ring_first(0)
    ffn(1)
    ring_first(1)

    ring_second(0)
    ring_second(1)
    ring_third(0)
    ring_third(1)
    ring_last(0)
    ring_last(1)
    for gather in (tok, kv, wo, res):
        gather.drain()
    for copy in core_sent + swaps + ring_sent:
        copy.wait_send()
    for store in stores:
        store.wait()


def cache_kernel(lengths, page_table, k_all, v_all, cache, k_win, v_win, sem):
    me = lax.axis_index("seq")

    def find(l, found):
        page = page_table[l]
        return tuple(jnp.where(page == me * PAGES_DEV + p, l, f) for p, f in enumerate(found))

    found = lax.fori_loop(0, PAGES, find, (jnp.int32(-1),) * PAGES_DEV)
    starts, bases = [], []
    begin, base = jnp.int32(0), jnp.int32(0)
    for r in range(REQS):
        starts.append(begin)
        bases.append(base)
        begin = begin + lengths[r]
        base = base + (lengths[r] + PAGE - 1) // PAGE
    plans = []
    for p in range(PAGES_DEV):
        l = found[p]
        first, size = jnp.int32(0), jnp.int32(0)
        for r in range(REQS):
            offset = (l - bases[r]) * PAGE
            inside = jnp.logical_and(l >= bases[r], offset < lengths[r])
            first = jnp.where(inside, starts[r] + offset, first)
            size = jnp.where(inside, jnp.minimum(lengths[r] - offset, PAGE), size)
        window = jnp.minimum(first // 16 * 16, N_SEQ * T - 80)
        chunk = jnp.minimum(first // 128, N_SEQ * CH - 2)
        copies = [
            pltpu.make_async_copy(v_all.at[pl.ds(pl.multiple_of(window, 16), 80)], v_win.at[p], sem.at[p, 0]),
            pltpu.make_async_copy(k_all.at[pl.ds(chunk, 2)], k_win.at[p], sem.at[p, 1]),
        ]
        for copy in copies:
            copy.start()
        plans.append((first - window, first - chunk * 128, size, copies))
    sel_row = lax.broadcasted_iota(jnp.int32, (PAGE, 80), 0)
    sel_col = lax.broadcasted_iota(jnp.int32, (PAGE, 80), 1)
    key_row = lax.broadcasted_iota(jnp.int32, (PAGE, 256), 0)
    key_col = lax.broadcasted_iota(jnp.int32, (PAGE, 256), 1)
    for p, (v_shift, k_shift, size, copies) in enumerate(plans):
        for copy in copies:
            copy.wait()
        picked = jnp.logical_and(sel_col == sel_row + v_shift, sel_row < size)
        values = jnp.dot(jnp.where(picked, 1.0, 0.0).astype(BF16), v_win[p], preferred_element_type=F32)
        chosen = jnp.logical_and(key_col == key_row + k_shift, key_row < size)
        keys = jnp.concatenate([k_win[p, 0, pl.ds(0, 128), :], k_win[p, 1, pl.ds(0, 128), :]], axis=1)
        rows = lax.dot_general(
            jnp.where(chosen, 1.0, 0.0).astype(BF16), keys,
            (((1,), (1,)), ((), ())), preferred_element_type=F32,
        )
        cache[pl.ds(p * PAGE, PAGE)] = jnp.stack([rows, values], axis=1).astype(BF16)


N_SEMS = 96


def per_device(
    tokens, variate, positions, lengths, page_table, gain_attn, w_query, w_key, w_value, var_bias,
    w_out, gain_ffn, w_gate, w_up, w_down,
):
    half = jnp.arange(LANES, dtype=jnp.int32) % 32
    frequency = (10000.0 ** (-(half.astype(F32)) / 32.0)).reshape(1, LANES)
    vmem = pl.BlockSpec(memory_space=pltpu.VMEM)
    smem = pl.BlockSpec(memory_space=pltpu.SMEM)
    anywhere = pl.BlockSpec(memory_space=pl.ANY)
    buf = lambda *shape: pltpu.VMEM(shape, BF16)
    mixed, k_all, v_all = pl.pallas_call(
        kernel,
        out_shape=(
            jax.ShapeDtypeStruct((T, LANES), BF16),
            jax.ShapeDtypeStruct((N_SEQ, CH, KX, LANES), BF16),
            jax.ShapeDtypeStruct((N_SEQ * T, LANES), BF16),
        ),
        in_specs=[smem] * 3 + [vmem] * 6 + [anywhere] * 3 + [vmem] + [anywhere] * 3,
        out_specs=(vmem, anywhere, anywhere),
        scratch_shapes=[
            buf(N_TP, T, LANES),
            buf(1024, 384),
            buf(N_SEQ, CH, KX, LANES),
            buf(N_SEQ * T, LANES),
            buf(2 * T, KX),
            pltpu.VMEM((2 * T, LANES), F32),
            pltpu.VMEM((2 * T, 2 * LANES), F32),
            buf(N_TP, LANES, 1024),
            buf(N_TP, 64, LANES),
            buf(N_TP, 64, LANES),
            buf(N_TP, 64, 1024),
            buf(T, 1024),
            buf(1024, T),
            buf(1024, T),
            buf(T, 1024),
            buf(N_TP, T, LANES),
            buf(2, 2, 2, 128, LANES),
            buf(2, 2, 2, 2, 128, LANES),
            buf(2, 2, 2, 128, LANES),
            buf(2, 256, LANES),
            buf(2, 256, LANES),
            pltpu.VMEM((2, T, LANES), F32),
            pltpu.SemaphoreType.DMA((N_SEMS,)),
            pltpu.SemaphoreType.DMA((N_SEMS,)),
            pltpu.SemaphoreType.DMA((8,)),
        ],
        compiler_params=pltpu.CompilerParams(collective_id=0, has_side_effects=True),
        name="layer",
    )(
        lengths, page_table, var_bias, tokens, variate.reshape(CH, LANES), positions.reshape(CH, LANES), frequency,
        gain_attn.reshape(1, 1024), gain_ffn.reshape(1, 1024), w_query, w_key, w_value, w_out, w_gate, w_up, w_down,
    )
    cache = pl.pallas_call(
        cache_kernel,
        out_shape=jax.ShapeDtypeStruct((PAGES_DEV * PAGE, 2, LANES), BF16),
        in_specs=[smem] * 2 + [anywhere] * 2,
        out_specs=vmem,
        scratch_shapes=[
            buf(PAGES_DEV, 2, KX, LANES),
            buf(PAGES_DEV, 80, LANES),
            pltpu.SemaphoreType.DMA((PAGES_DEV, 2)),
        ],
        name="pages",
    )(lengths, page_table, k_all.reshape(N_SEQ * CH, KX, LANES), v_all)
    return mixed, cache


def solution(mesh):
    placed = (
        P("seq", "tp"), P("seq"), P("seq"), P(), P(), P(), P(None, "tp"), P(None, "tp"), P(None, "tp"),
        P(None, "tp"), P("tp", None), P(), P(None, "tp"), P(None, "tp"), P("tp", None),
    )
    return jax.shard_map(
        per_device,
        mesh=mesh,
        in_specs=placed,
        out_specs=(P("seq", "tp"), P("seq", None, "tp")),
        check_vma=False,
    )
```

```python
import math

import jax
import jax.numpy as jnp
from jax import lax
from jax.experimental import pallas as pl
from jax.experimental.pallas import tpu as pltpu
from jax.sharding import PartitionSpec as P

MESH = pl.DeviceIdType.MESH
F32 = jnp.float32
BF16 = jnp.bfloat16
NEG = -1e30

T = 512
LANES = 128
CH = 4
KX = 144
N_SEQ = 16
N_TP = 8
PAGE = 64
PAGES_DEV = 9
PAGES = 144
REQS = 4


class Gather:
    COUNT = 14

    def __init__(self, own, part, slot, ring, pair, to_next, to_prev, to_pair, sems, base):
        self.own, self.part, self.slot = own, part, slot
        self.ring, self.pair = ring, pair
        self.targets = {"next": to_next, "prev": to_prev, "pair": to_pair}
        self.send, self.recv = sems
        self.base = base
        self.sent = []

    def at(self, dr, flip):
        ring = lax.rem(self.ring + (dr + 4), 4)
        return self.slot(ring, 1 - self.pair if flip else self.pair)

    def push(self, k, source, place, which, target):
        copy = pltpu.make_async_remote_copy(
            src_ref=source,
            dst_ref=self.part(place, which),
            send_sem=self.send.at[self.base + k],
            recv_sem=self.recv.at[self.base + k],
            device_id=self.targets[target],
            device_id_type=MESH,
        )
        copy.start()
        self.sent.append(copy)

    def wait(self, k, dr, flip, which):
        ref = self.part(self.at(dr, flip), which)
        pltpu.make_async_remote_copy(
            src_ref=ref,
            dst_ref=ref,
            send_sem=self.send.at[self.base + k],
            recv_sem=self.recv.at[self.base + k],
            device_id=self.targets["pair"],
            device_id_type=MESH,
        ).wait_recv()

    def start(self):
        mine = self.at(0, False)
        for which in (0, 1):
            self.push(which, self.own(which), mine, which, "pair")
        for which in (0, 1):
            self.push(2 + which, self.own(which), mine, which, "next")
            self.push(5 - which, self.own(1 - which), mine, 1 - which, "prev")

    def relay_pair(self):
        place = self.at(0, True)
        for which in (0, 1):
            self.wait(which, 0, True, which)
            self.push(6 + which, self.part(place, which), place, which, "next")
            self.push(8 + which, self.part(place, which), place, which, "prev")

    def relay_ring(self, flip):
        first = 6 if flip else 2
        onward = 12 if flip else 10
        before, after = self.at(-1, flip), self.at(1, flip)
        self.wait(first, -1, flip, 0)
        self.push(onward, self.part(before, 0), before, 0, "next")
        self.wait(first + 3, 1, flip, 1)
        self.push(onward + 1, self.part(after, 1), after, 1, "prev")
        self.wait(first + 1, -1, flip, 1)
        self.wait(first + 2, 1, flip, 0)

    def finish(self, flip):
        onward = 12 if flip else 10
        self.wait(onward, 2, flip, 0)
        self.wait(onward + 1, 2, flip, 1)

    def drain(self):
        for copy in self.sent:
            copy.wait_send()


def spread(row):
    return jnp.broadcast_to(row, (LANES, LANES)).T


def kernel(
    lengths,
    page_table,
    var_bias,
    tokens,
    variate,
    positions,
    gain_attn,
    gain_ffn,
    w_query,
    w_key,
    w_value,
    w_out,
    w_gate,
    w_up,
    w_down,
    mixed,
    k_all,
    v_all,
    tok_buf,
    w_qkv,
    kbuf,
    vbuf,
    qbuf,
    peak,
    acc,
    wout_buf,
    att_own,
    att_buf,
    res_buf,
    normed_buf,
    gate_buf,
    up_buf,
    down_buf,
    part_buf,
    hop_buf,
    near_buf,
    sum_buf,
    pair_tx,
    pair_rx,
    table,
    send_sem,
    recv_sem,
    load_sem,
):
    sems = (send_sem, recv_sem)
    me = lax.axis_index("seq")
    tp = lax.axis_index("tp")
    y, xl, core = me // 4, lax.rem(me // 2, 2), lax.rem(me, 2)
    z, xh = tp // 2, lax.rem(tp, 2)

    def seq_of(ys, xs, cs):
        return ys * 4 + xs * 2 + cs

    tp_at = lambda t: {"seq": me, "tp": t}
    seq_at = lambda s: {"seq": s, "tp": tp}
    z_next, z_prev = lax.rem(z + 1, 4), lax.rem(z + 3, 4)
    y_next, y_prev = lax.rem(y + 1, 4), lax.rem(y + 3, 4)

    loads = [
        pltpu.make_async_copy(w_query, w_qkv.at[:, pl.ds(0, 128)], load_sem.at[0]),
        pltpu.make_async_copy(w_key, w_qkv.at[:, pl.ds(128, 128)], load_sem.at[1]),
        pltpu.make_async_copy(w_value, w_qkv.at[:, pl.ds(256, 128)], load_sem.at[2]),
        pltpu.make_async_copy(w_gate, gate_buf, load_sem.at[3]),
        pltpu.make_async_copy(w_up, up_buf, load_sem.at[4]),
        pltpu.make_async_copy(w_down, down_buf, load_sem.at[5]),
    ]
    for load in loads:
        load.start()

    barrier = pltpu.get_barrier_semaphore()
    peers = [tp_at(lax.rem(tp + d, N_TP)) for d in range(1, N_TP)]
    peers += [
        seq_at(seq_of(y, xl, 1 - core)),
        seq_at(seq_of(y, 1 - xl, core)),
        seq_at(seq_of(y_next, xl, core)),
        seq_at(seq_of(y_prev, xl, core)),
    ]
    for peer in peers:
        pl.semaphore_signal(barrier, inc=1, device_id=peer, device_id_type=MESH)
    pl.semaphore_wait(barrier, len(peers))

    tp_targets = (tp_at(z_next * 2 + xh), tp_at(z_prev * 2 + xh), tp_at(z * 2 + 1 - xh))
    tp_slot = lambda r, p: r * 2 + p

    tok = Gather(
        lambda w: tokens.at[pl.ds(w * 256, 256)],
        lambda s, w: tok_buf.at[s, pl.ds(w * 256, 256)],
        tp_slot, z, xh, *tp_targets, sems, 0,
    )
    tok.start()
    tok_buf[tp] = tokens[...]

    lane = lax.broadcasted_iota(jnp.int32, (LANES, LANES), 1)
    low = lax.rem(lane, 64) < 32
    frequency = jnp.exp(lax.rem(lane, 32).astype(F32) * (-math.log(10000.0) / 32.0))
    for c in range(CH):
        angles = spread(positions[pl.ds(c, 1), :].astype(F32)) * frequency
        rows = pl.ds(c * 128, 128)
        table[0, rows, :] = jnp.cos(angles)
        sine = jnp.sin(angles)
        table[1, rows, :] = jnp.where(low, -sine, sine)

    tok.relay_ring(False)
    tok.relay_pair()
    tok.relay_ring(True)
    tok.finish(False)
    tok.finish(True)
    for load in loads[:3]:
        load.wait()

    ends = []
    total = jnp.int32(0)
    for r in range(REQS):
        total = total + lengths[r]
        ends.append(total)
    gains = [gain_attn[pl.ds(t, 1), :].astype(F32) for t in range(N_TP)]

    def segments(index):
        count = jnp.zeros(index.shape, jnp.int32)
        for end in ends:
            count += jnp.where(index >= end, 1, 0)
        return count

    sub16 = lax.broadcasted_iota(jnp.int32, (16, LANES), 0)
    lane16 = lax.broadcasted_iota(jnp.int32, (16, LANES), 1)
    sub = lax.broadcasted_iota(jnp.int32, (LANES, LANES), 0)
    first_head = lane < 64

    def project(c, _):
        rows = pl.ds(pl.multiple_of(c * 128, 128), 128)
        blocks = [tok_buf[t, rows, :].astype(F32) for t in range(N_TP)]
        squares = blocks[0] * blocks[0]
        for block in blocks[1:]:
            squares += block * block
        scale = lax.rsqrt(jnp.sum(squares, axis=1, keepdims=True) * (1.0 / 1024) + 1e-6)
        normed = jnp.concatenate([(b * scale * g).astype(BF16) for b, g in zip(blocks, gains)], axis=1)
        out = jnp.dot(normed, w_qkv[...], preferred_element_type=F32)
        cosine, sine = table[0, rows, :], table[1, rows, :]

        def rope(u):
            partner = jnp.where(low, pltpu.roll(u, 96, 1), pltpu.roll(u, 32, 1))
            return (u * cosine + partner * sine).astype(BF16)

        query = rope(out[:, :128]).astype(F32) * 0.125
        keys = rope(out[:, 128:256])
        kbuf[me, c, pl.ds(0, 128), :] = keys.astype(F32).T.astype(BF16)
        vbuf[pl.ds(pl.multiple_of(me * T + c * 128, 128), 128), :] = out[:, 256:].astype(BF16)

        vrow = variate[pl.ds(c, 1), :]
        kseg = segments(me * T + c * 128 + lane16)
        vb = jnp.broadcast_to(vrow, (16, LANES))
        code = jnp.where(sub16 < 8, lax.rem(sub16, 4) - vb, kseg + 8 - sub16)
        kbuf[me, c, pl.ds(128, 16), :] = jnp.where(code == 0, 1.0, 0.0).astype(BF16)

        vcol = spread(vrow.astype(F32)).astype(jnp.int32)
        qseg = segments(me * T + c * 128 + sub)
        seg_part = jnp.where(qseg == lane - 8, 0.0, jnp.where(lane < 12, NEG, 0.0))
        for h in range(2):
            weight = jnp.where(vcol == lax.rem(lane, 4), var_bias[0, h], var_bias[1, h])
            head = weight.astype(BF16).astype(F32)
            extra = jnp.where(lane < 4, head, jnp.where(lane < 8, weight - head, seg_part))
            own = first_head if h == 0 else jnp.logical_not(first_head)
            place = pl.ds(pl.multiple_of(h * T + c * 128, 128), 128)
            qbuf[place, pl.ds(0, 128)] = jnp.where(own, query, 0.0).astype(BF16)
            qbuf[place, pl.ds(128, 16)] = extra[:, :16].astype(BF16)
        return 0

    lax.fori_loop(0, CH, project, 0)

    def kv_part(s, w):
        return kbuf.at[s] if w == 0 else vbuf.at[pl.ds(pl.multiple_of(s * T, T), T)]

    kv = Gather(
        lambda w: kv_part(me, w), kv_part,
        lambda r, p: seq_of(r, p, core), y, xl,
        seq_at(seq_of(y_next, xl, core)), seq_at(seq_of(y_prev, xl, core)), seq_at(seq_of(y, 1 - xl, core)),
        sems, 14,
    )
    core_base = 28
    core_sent = []

    def core_copy(k, s, w):
        ref = kv_part(s, w)
        return pltpu.make_async_remote_copy(
            src_ref=ref, dst_ref=ref,
            send_sem=send_sem.at[core_base + k], recv_sem=recv_sem.at[core_base + k],
            device_id=seq_at(seq_of(y, xl, 1 - core)), device_id_type=MESH,
        )

    order = [(0, False), (0, True), (-1, False), (1, False), (-1, True), (1, True), (2, False), (2, True)]

    def place_of(dr, flip, cs):
        return seq_of(lax.rem(y + dr + 4, 4), (1 - xl) if flip else xl, cs)

    def core_send(n):
        s = place_of(*order[n], core)
        for w in (0, 1):
            copy = core_copy(n * 2 + w, s, w)
            copy.start()
            core_sent.append(copy)

    def core_wait(n):
        s = place_of(*order[n], 1 - core)
        for w in (0, 1):
            core_copy(n * 2 + w, s, w).wait_recv()

    core_send(0)
    kv.start()

    wo = Gather(
        lambda w: w_out.at[pl.ds(w * 64, 64)],
        lambda s, w: wout_buf.at[s, pl.ds(w * 64, 64)],
        tp_slot, z, xh, *tp_targets, sems, 44,
    )
    wo.start()
    wout_buf[tp] = w_out[...]

    ones = jnp.ones((T, LANES), BF16)

    def attend(s, diagonal):
        keys = jnp.concatenate([kbuf[s, c] for c in range(CH)], axis=1)
        values = jnp.concatenate([vbuf[pl.ds(pl.multiple_of(s * T, T), T), :], ones], axis=1)

        def tile(i, _):
            for h in range(2):
                rows = pl.ds(pl.multiple_of(h * T + i * 128, 128), 128)
                score = jnp.dot(qbuf[rows, :], keys, preferred_element_type=F32)
                if diagonal:
                    qi = i * 128 + lax.broadcasted_iota(jnp.int32, (128, T), 0)
                    ki = lax.broadcasted_iota(jnp.int32, (128, T), 1)
                    score = jnp.where(ki <= qi, score, NEG)
                    top = jnp.broadcast_to(jnp.max(score, axis=1, keepdims=True), (128, LANES))
                else:
                    before = peak[rows, :]
                    top = jnp.maximum(before, jnp.max(score, axis=1, keepdims=True))
                weight = jnp.exp(score - jnp.concatenate([top] * CH, axis=1)).astype(BF16)
                product = jnp.dot(weight, values, preferred_element_type=F32)
                if not diagonal:
                    fade = jnp.exp(before - top)
                    product += acc[rows, :] * jnp.concatenate([fade, fade], axis=1)
                acc[rows, :] = product
                peak[rows, :] = top
            return 0

        lax.fori_loop(0, CH, tile, 0, unroll=2)

    def attend_if(n, cs):
        s = place_of(*order[n], cs)

        @pl.when(jnp.logical_and(s < me, s >= me - 8))
        def _():
            attend(s, False)

    attend(me, True)
    core_wait(0)
    attend_if(0, 1 - core)
    kv.relay_pair()
    core_send(1)
    kv.relay_ring(False)
    core_send(2)
    core_send(3)
    wo.relay_pair()
    attend_if(1, core)
    attend_if(2, core)
    core_wait(1)
    core_wait(2)
    core_wait(3)
    wo.relay_ring(False)
    attend_if(1, 1 - core)
    attend_if(2, 1 - core)
    kv.relay_ring(True)
    core_send(4)
    core_send(5)
    wo.relay_ring(True)
    attend_if(4, core)
    kv.finish(False)
    core_send(6)
    core_wait(4)
    core_wait(5)
    attend_if(4, 1 - core)
    attend_if(6, core)
    kv.finish(True)
    core_send(7)
    core_wait(6)
    attend_if(6, 1 - core)
    attend_if(7, core)
    core_wait(7)
    attend_if(7, 1 - core)

    stores = [
        pltpu.make_async_copy(kbuf, k_all, load_sem.at[6]),
        pltpu.make_async_copy(vbuf, v_all, load_sem.at[7]),
    ]
    for store in stores:
        store.start()

    for c in range(CH):
        low_rows, high_rows = pl.ds(c * 128, 128), pl.ds(T + c * 128, 128)
        a, b = acc[low_rows, :], acc[high_rows, :]
        att = jnp.where(first_head, a[:, :128] / a[:, 128:], b[:, :128] / b[:, 128:]).astype(BF16)
        att_own[pl.ds(2 * c, 2)] = att.reshape(2, 64, 128)
    swap_base = 58
    swaps = []

    def swap(d, target, source_slot, place):
        return pltpu.make_async_remote_copy(
            src_ref=att_own.at[source_slot], dst_ref=att_buf.at[place],
            send_sem=send_sem.at[swap_base + d], recv_sem=recv_sem.at[swap_base + d],
            device_id=tp_at(target), device_id_type=MESH,
        )

    for d in (4, 3, 5, 2, 6, 1, 7):
        target = lax.rem(tp + d, N_TP)
        copy = swap(d, target, target, tp)
        copy.start()
        swaps.append(copy)
    att_buf[tp] = att_own[tp]
    wo.finish(False)
    wo.finish(True)
    for d in range(1, N_TP):
        origin = lax.rem(tp - d + N_TP, N_TP)
        swap(d, origin, origin, origin).wait_recv()
    rows_att = jnp.concatenate([att_buf[t] for t in range(N_TP)], axis=1)
    projected = jnp.dot(rows_att, wout_buf[...].reshape(1024, 1024), preferred_element_type=F32)
    own_rows = pl.ds(pl.multiple_of(tp * 64, 64), 64)
    own_tokens = jnp.concatenate([tok_buf[t, own_rows, :] for t in range(N_TP)], axis=1)
    res_buf[tp] = (own_tokens.astype(F32) + projected).astype(BF16)

    res = Gather(
        lambda w: res_buf.at[tp, pl.ds(w * 32, 32)],
        lambda s, w: res_buf.at[s, pl.ds(w * 32, 32)],
        tp_slot, z, xh, *tp_targets, sems, 66,
    )
    res.start()
    res.relay_ring(False)
    res.relay_pair()
    res.relay_ring(True)
    res.finish(False)
    res.finish(True)
    for load in loads[3:]:
        load.wait()

    ffn_gain = jnp.concatenate([gain_ffn[pl.ds(t, 1), :].astype(F32) for t in range(N_TP)], axis=1)

    def normalise(s, _):
        x = res_buf[s].astype(F32)
        scale = lax.rsqrt(jnp.sum(x * x, axis=1, keepdims=True) * (1.0 / 1024) + 1e-6)
        normed_buf[pl.ds(pl.multiple_of(s * 64, 64), 64), :] = (x * scale * ffn_gain).astype(BF16)
        return 0

    lax.fori_loop(0, N_TP, normalise, 0)

    ring_base = 80
    ring_sent = []

    def ring_copy(k, source, place, target):
        return pltpu.make_async_remote_copy(
            src_ref=source, dst_ref=place,
            send_sem=send_sem.at[ring_base + k], recv_sem=recv_sem.at[ring_base + k],
            device_id=target, device_id_type=MESH,
        )

    def ring_start(k, source, place, target):
        copy = ring_copy(k, source, place, target)
        copy.start()
        ring_sent.append(copy)

    z_far = lax.rem(z + 2, 4)
    next_at, prev_at, pair_at = tp_targets

    def pieces(zs, j, half):
        return part_buf.at[pl.ds(zs * 2, 2), pl.ds(j * 256 + half * 128, 128)]

    def ffn(j):
        rows = pl.ds(j * 256, 256)
        x = normed_buf[rows, :]
        gate = jnp.dot(x, gate_buf[...], preferred_element_type=F32)
        up = jnp.dot(x, up_buf[...], preferred_element_type=F32)
        hidden = (gate * (1.0 / (1.0 + jnp.exp(-gate))) * up).astype(BF16)
        for t in range(N_TP):
            part_buf[t, rows, :] = jnp.dot(
                hidden, down_buf[:, pl.ds(t * 128, 128)], preferred_element_type=F32
            ).astype(BF16)

    def ring_first(j):
        k = j * 8
        ring_start(k, pieces(z_far, j, 0), hop_buf.at[j, 0], next_at)
        ring_start(k + 1, pieces(z_far, j, 1), hop_buf.at[j, 1], prev_at)
        ring_start(k + 2, pieces(z_next, j, 1), near_buf.at[j, 0, 1], next_at)
        ring_start(k + 3, pieces(z_prev, j, 0), near_buf.at[j, 1, 0], prev_at)

    def ring_second(j):
        k = j * 8
        ring_copy(k, hop_buf.at[j, 0], hop_buf.at[j, 0], next_at).wait_recv()
        sum_buf[j, 0] = (hop_buf[j, 0].astype(F32) + pieces(z_next, j, 0)[...].astype(F32)).astype(BF16)
        ring_start(k + 4, sum_buf.at[j, 0], near_buf.at[j, 0, 0], next_at)
        ring_copy(k + 1, hop_buf.at[j, 1], hop_buf.at[j, 1], prev_at).wait_recv()
        sum_buf[j, 1] = (hop_buf[j, 1].astype(F32) + pieces(z_prev, j, 1)[...].astype(F32)).astype(BF16)
        ring_start(k + 5, sum_buf.at[j, 1], near_buf.at[j, 1, 1], prev_at)

    def own_sum(j, xs):
        total = []
        for half in (0, 1):
            own = part_buf[z * 2 + xs, pl.ds(j * 256 + half * 128, 128), :].astype(F32)
            total.append(own + near_buf[j, 0, half, xs].astype(F32) + near_buf[j, 1, half, xs].astype(F32))
        return jnp.concatenate(total, axis=0)

    def ring_third(j):
        k = j * 8
        ring_copy(k + 2, near_buf.at[j, 0, 1], near_buf.at[j, 0, 1], next_at).wait_recv()
        ring_copy(k + 3, near_buf.at[j, 1, 0], near_buf.at[j, 1, 0], prev_at).wait_recv()
        ring_copy(k + 4, near_buf.at[j, 0, 0], near_buf.at[j, 0, 0], next_at).wait_recv()
        ring_copy(k + 5, near_buf.at[j, 1, 1], near_buf.at[j, 1, 1], prev_at).wait_recv()
        pair_tx[j] = own_sum(j, 1 - xh).astype(BF16)
        ring_start(k + 6, pair_tx.at[j], pair_rx.at[j], pair_at)

    def ring_last(j):
        ring_copy(j * 8 + 6, pair_rx.at[j], pair_rx.at[j], pair_at).wait_recv()
        columns = pl.ds(pl.multiple_of(tp * 128, 128), 128)
        kept = jnp.concatenate([res_buf[4 * j + i, :, columns] for i in range(4)], axis=0).astype(F32)
        mixed[pl.ds(j * 256, 256), :] = (kept + own_sum(j, xh) + pair_rx[j].astype(F32)).astype(BF16)

    ffn(0)
    ring_first(0)
    ffn(1)
    ring_first(1)

    ring_second(0)
    ring_second(1)
    ring_third(0)
    ring_third(1)
    ring_last(0)
    ring_last(1)
    for gather in (tok, kv, wo, res):
        gather.drain()
    for copy in core_sent + swaps + ring_sent:
        copy.wait_send()
    for store in stores:
        store.wait()


def cache_kernel(lengths, page_table, k_all, v_all, cache, k_win, v_win, sem):
    me = lax.axis_index("seq")

    def find(l, found):
        page = page_table[l]
        return tuple(jnp.where(page == me * PAGES_DEV + p, l, f) for p, f in enumerate(found))

    found = lax.fori_loop(0, PAGES, find, (jnp.int32(-1),) * PAGES_DEV)
    starts, bases = [], []
    begin, base = jnp.int32(0), jnp.int32(0)
    for r in range(REQS):
        starts.append(begin)
        bases.append(base)
        begin = begin + lengths[r]
        base = base + (lengths[r] + PAGE - 1) // PAGE
    plans = []
    for p in range(PAGES_DEV):
        l = found[p]
        first, size = jnp.int32(0), jnp.int32(0)
        for r in range(REQS):
            offset = (l - bases[r]) * PAGE
            inside = jnp.logical_and(l >= bases[r], offset < lengths[r])
            first = jnp.where(inside, starts[r] + offset, first)
            size = jnp.where(inside, jnp.minimum(lengths[r] - offset, PAGE), size)
        window = jnp.minimum(first // 16 * 16, N_SEQ * T - 80)
        chunk = jnp.minimum(first // 128, N_SEQ * CH - 2)
        copies = [
            pltpu.make_async_copy(v_all.at[pl.ds(pl.multiple_of(window, 16), 80)], v_win.at[p], sem.at[p, 0]),
            pltpu.make_async_copy(k_all.at[pl.ds(chunk, 2)], k_win.at[p], sem.at[p, 1]),
        ]
        for copy in copies:
            copy.start()
        plans.append((first - window, first - chunk * 128, size, copies))
    sel_row = lax.broadcasted_iota(jnp.int32, (PAGE, 80), 0)
    sel_col = lax.broadcasted_iota(jnp.int32, (PAGE, 80), 1)
    key_row = lax.broadcasted_iota(jnp.int32, (PAGE, 256), 0)
    key_col = lax.broadcasted_iota(jnp.int32, (PAGE, 256), 1)
    for p, (v_shift, k_shift, size, copies) in enumerate(plans):
        for copy in copies:
            copy.wait()
        picked = jnp.logical_and(sel_col == sel_row + v_shift, sel_row < size)
        values = jnp.dot(jnp.where(picked, 1.0, 0.0).astype(BF16), v_win[p], preferred_element_type=F32)
        chosen = jnp.logical_and(key_col == key_row + k_shift, key_row < size)
        keys = jnp.concatenate([k_win[p, 0, pl.ds(0, 128), :], k_win[p, 1, pl.ds(0, 128), :]], axis=1)
        rows = lax.dot_general(
            jnp.where(chosen, 1.0, 0.0).astype(BF16), keys,
            (((1,), (1,)), ((), ())), preferred_element_type=F32,
        )
        cache[pl.ds(p * PAGE, PAGE)] = jnp.stack([rows, values], axis=1).astype(BF16)


N_SEMS = 96


def per_device(
    tokens, variate, positions, lengths, page_table, gain_attn, w_query, w_key, w_value, var_bias,
    w_out, gain_ffn, w_gate, w_up, w_down,
):
    vmem = pl.BlockSpec(memory_space=pltpu.VMEM)
    smem = pl.BlockSpec(memory_space=pltpu.SMEM)
    anywhere = pl.BlockSpec(memory_space=pl.ANY)
    buf = lambda *shape: pltpu.VMEM(shape, BF16)
    mixed, k_all, v_all = pl.pallas_call(
        kernel,
        out_shape=(
            jax.ShapeDtypeStruct((T, LANES), BF16),
            jax.ShapeDtypeStruct((N_SEQ, CH, KX, LANES), BF16),
            jax.ShapeDtypeStruct((N_SEQ * T, LANES), BF16),
        ),
        in_specs=[smem] * 3 + [vmem] * 5 + [anywhere] * 3 + [vmem] + [anywhere] * 3,
        out_specs=(vmem, anywhere, anywhere),
        scratch_shapes=[
            buf(N_TP, T, LANES),
            buf(1024, 384),
            buf(N_SEQ, CH, KX, LANES),
            buf(N_SEQ * T, LANES),
            buf(2 * T, KX),
            pltpu.VMEM((2 * T, LANES), F32),
            pltpu.VMEM((2 * T, 2 * LANES), F32),
            buf(N_TP, LANES, 1024),
            buf(N_TP, 64, LANES),
            buf(N_TP, 64, LANES),
            buf(N_TP, 64, 1024),
            buf(T, 1024),
            buf(1024, T),
            buf(1024, T),
            buf(T, 1024),
            buf(N_TP, T, LANES),
            buf(2, 2, 2, 128, LANES),
            buf(2, 2, 2, 2, 128, LANES),
            buf(2, 2, 2, 128, LANES),
            buf(2, 256, LANES),
            buf(2, 256, LANES),
            pltpu.VMEM((2, T, LANES), F32),
            pltpu.SemaphoreType.DMA((N_SEMS,)),
            pltpu.SemaphoreType.DMA((N_SEMS,)),
            pltpu.SemaphoreType.DMA((8,)),
        ],
        compiler_params=pltpu.CompilerParams(collective_id=0, has_side_effects=True),
        name="layer",
    )(
        lengths, page_table, var_bias, tokens, variate.reshape(CH, LANES), positions.reshape(CH, LANES),
        gain_attn.reshape(N_TP, LANES), gain_ffn.reshape(N_TP, LANES), w_query, w_key, w_value, w_out, w_gate, w_up, w_down,
    )
    cache = pl.pallas_call(
        cache_kernel,
        out_shape=jax.ShapeDtypeStruct((PAGES_DEV * PAGE, 2, LANES), BF16),
        in_specs=[smem] * 2 + [anywhere] * 2,
        out_specs=vmem,
        scratch_shapes=[
            buf(PAGES_DEV, 2, KX, LANES),
            buf(PAGES_DEV, 80, LANES),
            pltpu.SemaphoreType.DMA((PAGES_DEV, 2)),
        ],
        name="pages",
    )(lengths, page_table, k_all.reshape(N_SEQ * CH, KX, LANES), v_all)
    return mixed, cache


def solution(mesh):
    placed = (
        P("seq", "tp"), P("seq"), P("seq"), P(), P(), P(), P(None, "tp"), P(None, "tp"), P(None, "tp"),
        P(None, "tp"), P("tp", None), P(), P(None, "tp"), P(None, "tp"), P("tp", None),
    )
    return jax.shard_map(
        per_device,
        mesh=mesh,
        in_specs=placed,
        out_specs=(P("seq", "tp"), P("seq", None, "tp")),
        check_vma=False,
    )
```

```python
import math

import jax
import jax.numpy as jnp
from jax import lax
from jax.experimental import pallas as pl
from jax.experimental.pallas import tpu as pltpu
from jax.sharding import PartitionSpec as P

MESH = pl.DeviceIdType.MESH
F32 = jnp.float32
BF16 = jnp.bfloat16
NEG = -1e30

T = 512
LANES = 128
CH = 4
KX = 144
N_SEQ = 16
N_TP = 8
PAGE = 64
PAGES_DEV = 9
PAGES = 144
REQS = 4


class Gather:
    COUNT = 14

    def __init__(self, own, part, slot, ring, pair, to_next, to_prev, to_pair, sems, base):
        self.own, self.part, self.slot = own, part, slot
        self.ring, self.pair = ring, pair
        self.targets = {"next": to_next, "prev": to_prev, "pair": to_pair}
        self.send, self.recv = sems
        self.base = base
        self.sent = []

    def at(self, dr, flip):
        ring = lax.rem(self.ring + (dr + 4), 4)
        return self.slot(ring, 1 - self.pair if flip else self.pair)

    def push(self, k, source, place, which, target):
        copy = pltpu.make_async_remote_copy(
            src_ref=source,
            dst_ref=self.part(place, which),
            send_sem=self.send.at[self.base + k],
            recv_sem=self.recv.at[self.base + k],
            device_id=self.targets[target],
            device_id_type=MESH,
        )
        copy.start()
        self.sent.append(copy)

    def wait(self, k, dr, flip, which):
        ref = self.part(self.at(dr, flip), which)
        pltpu.make_async_remote_copy(
            src_ref=ref,
            dst_ref=ref,
            send_sem=self.send.at[self.base + k],
            recv_sem=self.recv.at[self.base + k],
            device_id=self.targets["pair"],
            device_id_type=MESH,
        ).wait_recv()

    def start(self):
        mine = self.at(0, False)
        for which in (0, 1):
            self.push(which, self.own(which), mine, which, "pair")
        for which in (0, 1):
            self.push(2 + which, self.own(which), mine, which, "next")
            self.push(5 - which, self.own(1 - which), mine, 1 - which, "prev")

    def relay_pair(self):
        place = self.at(0, True)
        for which in (0, 1):
            self.wait(which, 0, True, which)
            self.push(6 + which, self.part(place, which), place, which, "next")
            self.push(8 + which, self.part(place, which), place, which, "prev")

    def relay_ring(self, flip):
        first = 6 if flip else 2
        onward = 12 if flip else 10
        before, after = self.at(-1, flip), self.at(1, flip)
        self.wait(first, -1, flip, 0)
        self.push(onward, self.part(before, 0), before, 0, "next")
        self.wait(first + 3, 1, flip, 1)
        self.push(onward + 1, self.part(after, 1), after, 1, "prev")
        self.wait(first + 1, -1, flip, 1)
        self.wait(first + 2, 1, flip, 0)

    def finish(self, flip):
        onward = 12 if flip else 10
        self.wait(onward, 2, flip, 0)
        self.wait(onward + 1, 2, flip, 1)

    def drain(self):
        for copy in self.sent:
            copy.wait_send()


def spread(row):
    return jnp.broadcast_to(row, (LANES, LANES)).T


def kernel(
    lengths,
    page_table,
    var_bias,
    tokens,
    variate,
    positions,
    gain_attn,
    gain_ffn,
    w_query,
    w_key,
    w_value,
    w_out,
    w_gate,
    w_up,
    w_down,
    mixed,
    k_all,
    v_all,
    tok_buf,
    w_qkv,
    kbuf,
    vbuf,
    qbuf,
    peak,
    acc,
    wout_buf,
    att_buf,
    res_buf,
    normed_buf,
    gate_buf,
    up_buf,
    down_buf,
    part_buf,
    hop_buf,
    near_buf,
    sum_buf,
    pair_tx,
    pair_rx,
    table,
    send_sem,
    recv_sem,
    load_sem,
):
    sems = (send_sem, recv_sem)
    me = lax.axis_index("seq")
    tp = lax.axis_index("tp")
    y, xl, core = me // 4, lax.rem(me // 2, 2), lax.rem(me, 2)
    z, xh = tp // 2, lax.rem(tp, 2)

    def seq_of(ys, xs, cs):
        return ys * 4 + xs * 2 + cs

    tp_at = lambda t: {"seq": me, "tp": t}
    seq_at = lambda s: {"seq": s, "tp": tp}
    z_next, z_prev = lax.rem(z + 1, 4), lax.rem(z + 3, 4)
    y_next, y_prev = lax.rem(y + 1, 4), lax.rem(y + 3, 4)

    loads = [
        pltpu.make_async_copy(w_query, w_qkv.at[:, pl.ds(0, 128)], load_sem.at[0]),
        pltpu.make_async_copy(w_key, w_qkv.at[:, pl.ds(128, 128)], load_sem.at[1]),
        pltpu.make_async_copy(w_value, w_qkv.at[:, pl.ds(256, 128)], load_sem.at[2]),
        pltpu.make_async_copy(w_gate, gate_buf, load_sem.at[3]),
        pltpu.make_async_copy(w_up, up_buf, load_sem.at[4]),
        pltpu.make_async_copy(w_down, down_buf, load_sem.at[5]),
    ]
    for load in loads:
        load.start()

    barrier = pltpu.get_barrier_semaphore()
    peers = [tp_at(lax.rem(tp + d, N_TP)) for d in range(1, N_TP)]
    peers += [
        seq_at(seq_of(y, xl, 1 - core)),
        seq_at(seq_of(y, 1 - xl, core)),
        seq_at(seq_of(y_next, xl, core)),
        seq_at(seq_of(y_prev, xl, core)),
    ]
    for peer in peers:
        pl.semaphore_signal(barrier, inc=1, device_id=peer, device_id_type=MESH)
    pl.semaphore_wait(barrier, len(peers))

    tp_targets = (tp_at(z_next * 2 + xh), tp_at(z_prev * 2 + xh), tp_at(z * 2 + 1 - xh))
    tp_slot = lambda r, p: r * 2 + p

    tok = Gather(
        lambda w: tokens.at[pl.ds(w * 256, 256)],
        lambda s, w: tok_buf.at[s, pl.ds(w * 256, 256)],
        tp_slot, z, xh, *tp_targets, sems, 0,
    )
    tok.start()
    tok_buf[tp] = tokens[...]

    lane = lax.broadcasted_iota(jnp.int32, (LANES, LANES), 1)
    low = lax.rem(lane, 64) < 32
    frequency = jnp.exp(lax.rem(lane, 32).astype(F32) * (-math.log(10000.0) / 32.0))
    for c in range(CH):
        angles = spread(positions[pl.ds(c, 1), :].astype(F32)) * frequency
        rows = pl.ds(c * 128, 128)
        table[0, rows, :] = jnp.cos(angles)
        sine = jnp.sin(angles)
        table[1, rows, :] = jnp.where(low, -sine, sine)

    tok.relay_ring(False)
    tok.relay_pair()
    tok.relay_ring(True)
    tok.finish(False)
    tok.finish(True)
    for load in loads[:3]:
        load.wait()

    ends = []
    total = jnp.int32(0)
    for r in range(REQS):
        total = total + lengths[r]
        ends.append(total)
    gains = [gain_attn[pl.ds(t, 1), :].astype(F32) for t in range(N_TP)]

    def segments(index):
        count = jnp.zeros(index.shape, jnp.int32)
        for end in ends:
            count += jnp.where(index >= end, 1, 0)
        return count

    sub16 = lax.broadcasted_iota(jnp.int32, (16, LANES), 0)
    lane16 = lax.broadcasted_iota(jnp.int32, (16, LANES), 1)
    sub = lax.broadcasted_iota(jnp.int32, (LANES, LANES), 0)
    first_head = lane < 64

    def project(c, _):
        rows = pl.ds(pl.multiple_of(c * 128, 128), 128)
        blocks = [tok_buf[t, rows, :].astype(F32) for t in range(N_TP)]
        squares = blocks[0] * blocks[0]
        for block in blocks[1:]:
            squares += block * block
        scale = lax.rsqrt(jnp.sum(squares, axis=1, keepdims=True) * (1.0 / 1024) + 1e-6)
        normed = jnp.concatenate([(b * scale * g).astype(BF16) for b, g in zip(blocks, gains)], axis=1)
        out = jnp.dot(normed, w_qkv[...], preferred_element_type=F32)
        cosine, sine = table[0, rows, :], table[1, rows, :]

        def rope(u):
            partner = jnp.where(low, pltpu.roll(u, 96, 1), pltpu.roll(u, 32, 1))
            return (u * cosine + partner * sine).astype(BF16)

        query = rope(out[:, :128]).astype(F32) * 0.125
        keys = rope(out[:, 128:256])
        kbuf[me, c, pl.ds(0, 128), :] = keys.astype(F32).T.astype(BF16)
        vbuf[pl.ds(pl.multiple_of(me * T + c * 128, 128), 128), :] = out[:, 256:].astype(BF16)

        vrow = variate[pl.ds(c, 1), :]
        kseg = segments(me * T + c * 128 + lane16)
        vb = jnp.broadcast_to(vrow, (16, LANES))
        code = jnp.where(sub16 < 8, lax.rem(sub16, 4) - vb, kseg + 8 - sub16)
        kbuf[me, c, pl.ds(128, 16), :] = jnp.where(code == 0, 1.0, 0.0).astype(BF16)

        vcol = spread(vrow.astype(F32)).astype(jnp.int32)
        qseg = segments(me * T + c * 128 + sub)
        seg_part = jnp.where(qseg == lane - 8, 0.0, jnp.where(lane < 12, NEG, 0.0))
        for h in range(2):
            weight = jnp.where(vcol == lax.rem(lane, 4), var_bias[0, h], var_bias[1, h])
            head = weight.astype(BF16).astype(F32)
            extra = jnp.where(lane < 4, head, jnp.where(lane < 8, weight - head, seg_part))
            own = first_head if h == 0 else jnp.logical_not(first_head)
            place = pl.ds(pl.multiple_of(h * T + c * 128, 128), 128)
            qbuf[place, pl.ds(0, 128)] = jnp.where(own, query, 0.0).astype(BF16)
            qbuf[place, pl.ds(128, 16)] = extra[:, :16].astype(BF16)
        return 0

    lax.fori_loop(0, CH, project, 0)

    def kv_part(s, w):
        return kbuf.at[s] if w == 0 else vbuf.at[pl.ds(pl.multiple_of(s * T, T), T)]

    kv = Gather(
        lambda w: kv_part(me, w), kv_part,
        lambda r, p: seq_of(r, p, core), y, xl,
        seq_at(seq_of(y_next, xl, core)), seq_at(seq_of(y_prev, xl, core)), seq_at(seq_of(y, 1 - xl, core)),
        sems, 14,
    )
    core_base = 28
    core_sent = []

    def core_copy(k, s, w):
        ref = kv_part(s, w)
        return pltpu.make_async_remote_copy(
            src_ref=ref, dst_ref=ref,
            send_sem=send_sem.at[core_base + k], recv_sem=recv_sem.at[core_base + k],
            device_id=seq_at(seq_of(y, xl, 1 - core)), device_id_type=MESH,
        )

    order = [(0, False), (0, True), (-1, False), (1, False), (-1, True), (1, True), (2, False), (2, True)]

    def place_of(dr, flip, cs):
        return seq_of(lax.rem(y + dr + 4, 4), (1 - xl) if flip else xl, cs)

    def core_send(n):
        s = place_of(*order[n], core)
        for w in (0, 1):
            copy = core_copy(n * 2 + w, s, w)
            copy.start()
            core_sent.append(copy)

    def core_wait(n):
        s = place_of(*order[n], 1 - core)
        for w in (0, 1):
            core_copy(n * 2 + w, s, w).wait_recv()

    core_send(0)
    kv.start()

    wo = Gather(
        lambda w: w_out.at[pl.ds(w * 64, 64)],
        lambda s, w: wout_buf.at[s, pl.ds(w * 64, 64)],
        tp_slot, z, xh, *tp_targets, sems, 44,
    )
    wo.start()
    wout_buf[tp] = w_out[...]

    ones = jnp.ones((T, LANES), BF16)

    def attend(s, diagonal):
        keys = jnp.concatenate([kbuf[s, c] for c in range(CH)], axis=1)
        values = jnp.concatenate([vbuf[pl.ds(pl.multiple_of(s * T, T), T), :], ones], axis=1)

        def tile(i, _):
            for h in range(2):
                rows = pl.ds(pl.multiple_of(h * T + i * 128, 128), 128)
                score = jnp.dot(qbuf[rows, :], keys, preferred_element_type=F32)
                if diagonal:
                    qi = i * 128 + lax.broadcasted_iota(jnp.int32, (128, T), 0)
                    ki = lax.broadcasted_iota(jnp.int32, (128, T), 1)
                    score = jnp.where(ki <= qi, score, NEG)
                    top = jnp.broadcast_to(jnp.max(score, axis=1, keepdims=True), (128, LANES))
                else:
                    before = peak[rows, :]
                    top = jnp.maximum(before, jnp.max(score, axis=1, keepdims=True))
                weight = jnp.exp(score - jnp.concatenate([top] * CH, axis=1)).astype(BF16)
                product = jnp.dot(weight, values, preferred_element_type=F32)
                if not diagonal:
                    fade = jnp.exp(before - top)
                    product += acc[rows, :] * jnp.concatenate([fade, fade], axis=1)
                acc[rows, :] = product
                peak[rows, :] = top
            return 0

        lax.fori_loop(0, CH, tile, 0, unroll=2)

    def attend_if(n, cs):
        s = place_of(*order[n], cs)

        @pl.when(jnp.logical_and(s < me, s >= me - 8))
        def _():
            attend(s, False)

    attend(me, True)
    core_wait(0)
    attend_if(0, 1 - core)
    kv.relay_pair()
    core_send(1)
    kv.relay_ring(False)
    core_send(2)
    core_send(3)
    wo.relay_pair()
    attend_if(1, core)
    attend_if(2, core)
    core_wait(1)
    core_wait(2)
    core_wait(3)
    wo.relay_ring(False)
    attend_if(1, 1 - core)
    attend_if(2, 1 - core)
    kv.relay_ring(True)
    core_send(4)
    core_send(5)
    wo.relay_ring(True)
    attend_if(4, core)
    kv.finish(False)
    core_send(6)
    core_wait(4)
    core_wait(5)
    attend_if(4, 1 - core)
    attend_if(6, core)
    kv.finish(True)
    core_send(7)
    core_wait(6)
    attend_if(6, 1 - core)
    attend_if(7, core)
    core_wait(7)
    attend_if(7, 1 - core)

    stores = [
        pltpu.make_async_copy(kbuf, k_all, load_sem.at[6]),
        pltpu.make_async_copy(vbuf, v_all, load_sem.at[7]),
    ]
    for store in stores:
        store.start()

    for c in range(CH):
        low_rows, high_rows = pl.ds(c * 128, 128), pl.ds(T + c * 128, 128)
        a, b = acc[low_rows, :], acc[high_rows, :]
        att_buf[tp, pl.ds(c * 128, 128), :] = jnp.where(
            first_head, a[:, :128] / a[:, 128:], b[:, :128] / b[:, 128:]
        ).astype(BF16)
    att = Gather(
        lambda w: att_buf.at[tp, pl.ds(w * 256, 256)],
        lambda s, w: att_buf.at[s, pl.ds(w * 256, 256)],
        tp_slot, z, xh, *tp_targets, sems, 66,
    )
    att.start()
    wo.finish(False)
    wo.finish(True)
    att.relay_ring(False)
    att.relay_pair()
    att.relay_ring(True)
    att.finish(False)
    att.finish(True)
    for load in loads[3:]:
        load.wait()

    ffn_gain = jnp.concatenate([gain_ffn[pl.ds(t, 1), :].astype(F32) for t in range(N_TP)], axis=1)

    def residual(j):
        rows = pl.ds(j * 256, 256)
        attended = jnp.concatenate([att_buf[t, rows, :] for t in range(N_TP)], axis=1)
        projected = jnp.dot(attended, wout_buf[...].reshape(1024, 1024), preferred_element_type=F32)
        held = jnp.concatenate([tok_buf[t, rows, :] for t in range(N_TP)], axis=1).astype(F32)
        rounded = (held + projected).astype(BF16)
        res_buf[rows, :] = rounded
        x = rounded.astype(F32)
        scale = lax.rsqrt(jnp.sum(x * x, axis=1, keepdims=True) * (1.0 / 1024) + 1e-6)
        normed_buf[rows, :] = (x * scale * ffn_gain).astype(BF16)

    ring_base = 80
    ring_sent = []

    def ring_copy(k, source, place, target):
        return pltpu.make_async_remote_copy(
            src_ref=source, dst_ref=place,
            send_sem=send_sem.at[ring_base + k], recv_sem=recv_sem.at[ring_base + k],
            device_id=target, device_id_type=MESH,
        )

    def ring_start(k, source, place, target):
        copy = ring_copy(k, source, place, target)
        copy.start()
        ring_sent.append(copy)

    z_far = lax.rem(z + 2, 4)
    next_at, prev_at, pair_at = tp_targets

    def pieces(zs, j, half):
        return part_buf.at[pl.ds(zs * 2, 2), pl.ds(j * 256 + half * 128, 128)]

    def ffn(j):
        rows = pl.ds(j * 256, 256)
        x = normed_buf[rows, :]
        gate = jnp.dot(x, gate_buf[...], preferred_element_type=F32)
        up = jnp.dot(x, up_buf[...], preferred_element_type=F32)
        hidden = (gate * (1.0 / (1.0 + jnp.exp(-gate))) * up).astype(BF16)
        for t in range(N_TP):
            part_buf[t, rows, :] = jnp.dot(
                hidden, down_buf[:, pl.ds(t * 128, 128)], preferred_element_type=F32
            ).astype(BF16)

    def ring_first(j):
        k = j * 8
        ring_start(k, pieces(z_far, j, 0), hop_buf.at[j, 0], next_at)
        ring_start(k + 1, pieces(z_far, j, 1), hop_buf.at[j, 1], prev_at)
        ring_start(k + 2, pieces(z_next, j, 1), near_buf.at[j, 0, 1], next_at)
        ring_start(k + 3, pieces(z_prev, j, 0), near_buf.at[j, 1, 0], prev_at)

    def ring_second(j):
        k = j * 8
        ring_copy(k, hop_buf.at[j, 0], hop_buf.at[j, 0], next_at).wait_recv()
        sum_buf[j, 0] = (hop_buf[j, 0].astype(F32) + pieces(z_next, j, 0)[...].astype(F32)).astype(BF16)
        ring_start(k + 4, sum_buf.at[j, 0], near_buf.at[j, 0, 0], next_at)
        ring_copy(k + 1, hop_buf.at[j, 1], hop_buf.at[j, 1], prev_at).wait_recv()
        sum_buf[j, 1] = (hop_buf[j, 1].astype(F32) + pieces(z_prev, j, 1)[...].astype(F32)).astype(BF16)
        ring_start(k + 5, sum_buf.at[j, 1], near_buf.at[j, 1, 1], prev_at)

    def own_sum(j, xs):
        total = []
        for half in (0, 1):
            own = part_buf[z * 2 + xs, pl.ds(j * 256 + half * 128, 128), :].astype(F32)
            total.append(own + near_buf[j, 0, half, xs].astype(F32) + near_buf[j, 1, half, xs].astype(F32))
        return jnp.concatenate(total, axis=0)

    def ring_third(j):
        k = j * 8
        ring_copy(k + 2, near_buf.at[j, 0, 1], near_buf.at[j, 0, 1], next_at).wait_recv()
        ring_copy(k + 3, near_buf.at[j, 1, 0], near_buf.at[j, 1, 0], prev_at).wait_recv()
        ring_copy(k + 4, near_buf.at[j, 0, 0], near_buf.at[j, 0, 0], next_at).wait_recv()
        ring_copy(k + 5, near_buf.at[j, 1, 1], near_buf.at[j, 1, 1], prev_at).wait_recv()
        pair_tx[j] = own_sum(j, 1 - xh).astype(BF16)
        ring_start(k + 6, pair_tx.at[j], pair_rx.at[j], pair_at)

    def ring_last(j):
        ring_copy(j * 8 + 6, pair_rx.at[j], pair_rx.at[j], pair_at).wait_recv()
        columns = pl.ds(pl.multiple_of(tp * 128, 128), 128)
        kept = res_buf[pl.ds(j * 256, 256), columns].astype(F32)
        mixed[pl.ds(j * 256, 256), :] = (kept + own_sum(j, xh) + pair_rx[j].astype(F32)).astype(BF16)

    residual(0)
    ffn(0)
    ring_first(0)
    residual(1)
    ffn(1)
    ring_first(1)

    ring_second(0)
    ring_second(1)
    ring_third(0)
    ring_third(1)
    ring_last(0)
    ring_last(1)
    for gather in (tok, kv, wo, att):
        gather.drain()
    for copy in core_sent + ring_sent:
        copy.wait_send()
    for store in stores:
        store.wait()


def cache_kernel(lengths, page_table, k_all, v_all, cache, k_win, v_win, sem):
    me = lax.axis_index("seq")

    def find(l, found):
        page = page_table[l]
        return tuple(jnp.where(page == me * PAGES_DEV + p, l, f) for p, f in enumerate(found))

    found = lax.fori_loop(0, PAGES, find, (jnp.int32(-1),) * PAGES_DEV, unroll=8)
    starts, bases = [], []
    begin, base = jnp.int32(0), jnp.int32(0)
    for r in range(REQS):
        starts.append(begin)
        bases.append(base)
        begin = begin + lengths[r]
        base = base + (lengths[r] + PAGE - 1) // PAGE
    plans = []
    for p in range(PAGES_DEV):
        l = found[p]
        first, size = jnp.int32(0), jnp.int32(0)
        for r in range(REQS):
            offset = (l - bases[r]) * PAGE
            inside = jnp.logical_and(l >= bases[r], offset < lengths[r])
            first = jnp.where(inside, starts[r] + offset, first)
            size = jnp.where(inside, jnp.minimum(lengths[r] - offset, PAGE), size)
        window = jnp.minimum(first // 16 * 16, N_SEQ * T - 80)
        chunk = jnp.minimum(first // 128, N_SEQ * CH - 2)
        copies = [
            pltpu.make_async_copy(v_all.at[pl.ds(pl.multiple_of(window, 16), 80)], v_win.at[p], sem.at[p, 0]),
            pltpu.make_async_copy(k_all.at[pl.ds(chunk, 2)], k_win.at[p], sem.at[p, 1]),
        ]
        for copy in copies:
            copy.start()
        plans.append((first - window, first - chunk * 128, size, copies))
    sel_row = lax.broadcasted_iota(jnp.int32, (PAGE, 80), 0)
    sel_col = lax.broadcasted_iota(jnp.int32, (PAGE, 80), 1)
    key_row = lax.broadcasted_iota(jnp.int32, (PAGE, 256), 0)
    key_col = lax.broadcasted_iota(jnp.int32, (PAGE, 256), 1)
    for p, (v_shift, k_shift, size, copies) in enumerate(plans):
        for copy in copies:
            copy.wait()
        picked = jnp.logical_and(sel_col == sel_row + v_shift, sel_row < size)
        values = jnp.dot(jnp.where(picked, 1.0, 0.0).astype(BF16), v_win[p], preferred_element_type=F32)
        chosen = jnp.logical_and(key_col == key_row + k_shift, key_row < size)
        keys = jnp.concatenate([k_win[p, 0, pl.ds(0, 128), :], k_win[p, 1, pl.ds(0, 128), :]], axis=1)
        rows = lax.dot_general(
            jnp.where(chosen, 1.0, 0.0).astype(BF16), keys,
            (((1,), (1,)), ((), ())), preferred_element_type=F32,
        )
        cache[pl.ds(p * PAGE, PAGE)] = jnp.stack([rows, values], axis=1).astype(BF16)


N_SEMS = 96


def per_device(
    tokens, variate, positions, lengths, page_table, gain_attn, w_query, w_key, w_value, var_bias,
    w_out, gain_ffn, w_gate, w_up, w_down,
):
    vmem = pl.BlockSpec(memory_space=pltpu.VMEM)
    smem = pl.BlockSpec(memory_space=pltpu.SMEM)
    anywhere = pl.BlockSpec(memory_space=pl.ANY)
    buf = lambda *shape: pltpu.VMEM(shape, BF16)
    mixed, k_all, v_all = pl.pallas_call(
        kernel,
        out_shape=(
            jax.ShapeDtypeStruct((T, LANES), BF16),
            jax.ShapeDtypeStruct((N_SEQ, CH, KX, LANES), BF16),
            jax.ShapeDtypeStruct((N_SEQ * T, LANES), BF16),
        ),
        in_specs=[smem] * 3 + [vmem] * 5 + [anywhere] * 3 + [vmem] + [anywhere] * 3,
        out_specs=(vmem, anywhere, anywhere),
        scratch_shapes=[
            buf(N_TP, T, LANES),
            buf(1024, 384),
            buf(N_SEQ, CH, KX, LANES),
            buf(N_SEQ * T, LANES),
            buf(2 * T, KX),
            pltpu.VMEM((2 * T, LANES), F32),
            pltpu.VMEM((2 * T, 2 * LANES), F32),
            buf(N_TP, LANES, 1024),
            buf(N_TP, T, LANES),
            buf(T, 1024),
            buf(T, 1024),
            buf(1024, T),
            buf(1024, T),
            buf(T, 1024),
            buf(N_TP, T, LANES),
            buf(2, 2, 2, 128, LANES),
            buf(2, 2, 2, 2, 128, LANES),
            buf(2, 2, 2, 128, LANES),
            buf(2, 256, LANES),
            buf(2, 256, LANES),
            pltpu.VMEM((2, T, LANES), F32),
            pltpu.SemaphoreType.DMA((N_SEMS,)),
            pltpu.SemaphoreType.DMA((N_SEMS,)),
            pltpu.SemaphoreType.DMA((8,)),
        ],
        compiler_params=pltpu.CompilerParams(collective_id=0, has_side_effects=True),
        name="layer",
    )(
        lengths, page_table, var_bias, tokens, variate.reshape(CH, LANES), positions.reshape(CH, LANES),
        gain_attn.reshape(N_TP, LANES), gain_ffn.reshape(N_TP, LANES), w_query, w_key, w_value, w_out, w_gate, w_up, w_down,
    )
    cache = pl.pallas_call(
        cache_kernel,
        out_shape=jax.ShapeDtypeStruct((PAGES_DEV * PAGE, 2, LANES), BF16),
        in_specs=[smem] * 2 + [anywhere] * 2,
        out_specs=vmem,
        scratch_shapes=[
            buf(PAGES_DEV, 2, KX, LANES),
            buf(PAGES_DEV, 80, LANES),
            pltpu.SemaphoreType.DMA((PAGES_DEV, 2)),
        ],
        name="pages",
    )(lengths, page_table, k_all.reshape(N_SEQ * CH, KX, LANES), v_all)
    return mixed, cache


def solution(mesh):
    placed = (
        P("seq", "tp"), P("seq"), P("seq"), P(), P(), P(), P(None, "tp"), P(None, "tp"), P(None, "tp"),
        P(None, "tp"), P("tp", None), P(), P(None, "tp"), P(None, "tp"), P("tp", None),
    )
    return jax.shard_map(
        per_device,
        mesh=mesh,
        in_specs=placed,
        out_specs=(P("seq", "tp"), P("seq", None, "tp")),
        check_vma=False,
    )
```
